32 devices in a mesh: seq: 4 (over y, core), chan: 8 (over z, x).
Axes of the slice: x: 2, y: 2, z: 4, core: 2. Of those that a mesh axis runs over, the one named last changes fastest.
Arguments:
- scan_input: bfloat16 [1024, 5120], P('seq', 'chan'), may hold values from -6 to 6
- gate_input: bfloat16 [1024, 5120], P('seq', 'chan'), may hold values from -6 to 6
- step_raw: bfloat16 [1024, 5120], P('seq', 'chan')
- log_rates: float32 [16, 5120], P(None, 'chan')
- skip_gain: float32 [5120], P('chan'), may hold values from 0.5 to 1.5
- state_write: float32 [16, 1024], P(None, 'seq'), may hold values from -6 to 6
- state_read: float32 [16, 1024], P(None, 'seq'), may hold values from -6 to 6
- out_weight: bfloat16 [5120, 2560], P('chan'), may hold values from -0.078125 to 0.078125
- out_cotangent: bfloat16 [1024, 2560], P('seq', 'chan'), may hold values from -6 to 6
Outputs:
- grad_input: bfloat16 [1024, 5120], P('seq', 'chan')
- grad_gate: bfloat16 [1024, 5120], P('seq', 'chan')
- grad_step: bfloat16 [1024, 5120], P('seq', 'chan')
- grad_rates: float32 [16, 5120], P(None, 'chan')
- grad_skip: float32 [5120], P('chan')
- grad_write: float32 [16, 1024], P(None, ('seq', 'chan'))
- grad_read: float32 [16, 1024], P(None, ('seq', 'chan'))
- grad_weight: float32 [5120, 2560], P('chan', 'seq')
The draws below stay inside these ranges and needn't reach their ends.
All inputs are finite; a program needn't handle non-finite values.
Results may differ from the reference program's by a relative error of at most 0.0095.
Values may be sent and summed in bfloat16 or wider, within the bound.
A program may use at most 64 MiB of HBM per device.

```python
import jax
import jax.numpy as jnp
from jax import lax

DM = 2560
EI = 5120
DS = 16
TOKENS = 1024
N_CHAN = 8


def draw_log_rates(key, part):
    first, second = jax.random.split(key, 2)
    root = jnp.sqrt(jnp.float32(TOKENS))
    share = 0.5
    quick = jax.random.uniform(first, (DS, EI), jnp.float32) < share
    spread = jax.random.uniform(second, (DS, EI), jnp.float32)
    slow_rate = 0.2 / root * jnp.power(10.0, spread)
    quick_rate = root / 40.0 * jnp.power(10.0, spread)
    return jnp.log(jnp.where(quick, quick_rate, slow_rate)).astype(jnp.float32)


def draw_step_raw(key, part):
    root = jnp.sqrt(jnp.float32(TOKENS))
    spread = jax.random.uniform(key, (TOKENS, EI), jnp.float32)
    target = 0.3 * jnp.power(10.0, spread) / root
    return jnp.log(jnp.expm1(target)).astype(jnp.bfloat16)


def with_spikes(values, stream_key, source, target, shards_of, factor):
    owner, partner = [(jnp.arange(values.shape[dim]) // (values.shape[dim] // shards_of)).reshape([-1 if axis == dim else 1 for axis in range(values.ndim)]) for dim in (source, target)]
    chosen = jax.random.permutation(stream_key, shards_of)[partner]
    strong = (owner == chosen) | (owner == (partner + shards_of // 2) % shards_of)
    return jnp.where(strong, factor * values, values)


def levels(stream_key, dims, cuts, least, largest):
    factor_of, own = 1.0, jax.random.fold_in(stream_key, 6)
    for position, parts in cuts:
        steps = jnp.exp(jax.random.uniform(jax.random.fold_in(own, position), (parts,), jnp.float32, least / len(cuts), largest / len(cuts)))
        factor_of = factor_of * jnp.repeat(steps, dims[position] // parts).reshape([-1 if axis == position else 1 for axis in range(len(dims))])
    return factor_of


def bell_draw(rng, extent, scale, most, cuts=(), kind=jnp.bfloat16):
    result = scale * jax.random.normal(rng, extent, jnp.float32)
    if cuts:
        result = result * levels(rng, extent, cuts, -0.22, 0.18)
    return jnp.clip(result, -most, most).astype(kind)


def bell_draw_with(own_key, shape, scale, limit, shards, heavy, kind=jnp.bfloat16):
    entries = scale * jax.random.normal(own_key, shape, jnp.float32)
    if shards:
        entries = entries * levels(own_key, shape, shards, -0.22, 0.18)
    return jnp.clip(with_spikes(entries, jax.random.fold_in(own_key, 3), *heavy), -limit, limit).astype(kind)


def setup_inputs(seed: int = 0) -> dict:
    key_list = jax.random.split(jax.random.key(seed), 10)
    return {
        "scan_input": bell_draw_with(key_list[0], (TOKENS, EI), 1.0, 6.0, ((0, 4), (1, 8)), (1, 0, 8, 2.0)),
        "gate_input": bell_draw(key_list[1], (TOKENS, EI), 1.0, 6.0, ((0, 4), (1, 8))),
        "step_raw": draw_step_raw(jax.random.fold_in(key_list[9], 71), 0),
        "log_rates": draw_log_rates(jax.random.fold_in(key_list[9], 71), 0),
        "skip_gain": jnp.clip(1.0 + 0.1 * jax.random.normal(key_list[4], (EI,), jnp.float32), 0.5, 1.5),
        "state_write": bell_draw(key_list[5], (DS, TOKENS), 1.0, 6.0, ((1, 4),), jnp.float32),
        "state_read": bell_draw(key_list[6], (DS, TOKENS), 1.0, 6.0, ((1, 4),), jnp.float32),
        "out_weight": bell_draw(key_list[7], (EI, DM), EI ** -0.5, 0.078125, ((0, 8),)),
        "out_cotangent": bell_draw_with(key_list[8], (TOKENS, DM), 1.0, 6.0, ((0, 4), (1, 8)), (0, 1, 8, 2.0)),
    }


def reference(scan_input, gate_input, step_raw, log_rates, skip_gain, state_write, state_read, out_weight, out_cotangent):
    width = EI // N_CHAN
    delta = jax.nn.softplus(step_raw.astype(jnp.float32))
    a_neg = -jnp.exp(log_rates)
    xf = scan_input.astype(jnp.float32)
    zf = gate_input.astype(jnp.float32)
    gate_sig = jax.nn.sigmoid(zf)
    gate_silu = zf * gate_sig
    dg = jnp.dot(out_cotangent, out_weight.T, preferred_element_type=jnp.float32)
    dy = dg * gate_silu
    b_rows = state_write.T
    c_rows = state_read.T

    def group(index):
        start = index * width
        x_g = lax.dynamic_slice_in_dim(xf, start, width, 1)
        d_g = lax.dynamic_slice_in_dim(delta, start, width, 1)
        a_g = lax.dynamic_slice_in_dim(a_neg, start, width, 1)
        dy_g = lax.dynamic_slice_in_dim(dy, start, width, 1)
        skip_g = lax.dynamic_slice_in_dim(skip_gain, start, width, 0)

        def forward(state, inputs):
            d_t, x_t, b_t = inputs
            state = jnp.exp(d_t[None, :] * a_g) * state + b_t[:, None] * (d_t * x_t)[None, :]
            return state, state

        zero_state = jnp.zeros((DS, width), jnp.float32)
        _, states = lax.scan(forward, zero_state, (d_g, x_g, b_rows))
        y_g = jnp.einsum("nt,tne->te", state_read, states) + skip_g[None, :] * x_g
        grad_c_part = jnp.einsum("te,tne->nt", dy_g, states)
        previous = jnp.concatenate([zero_state[None], states[:-1]], axis=0)

        def backward(carry, inputs):
            omega, acc = carry
            d_t, x_t, b_t, c_t, dy_t, prev_t = inputs
            dec = jnp.exp(d_t[None, :] * a_g)
            lam = c_t[:, None] * dy_t[None, :] + omega
            lam_b = jnp.sum(lam * b_t[:, None], axis=0)
            gdelta = x_t * lam_b + jnp.sum(lam * a_g * dec * prev_t, axis=0)
            gx = d_t * lam_b + dy_t * skip_g
            gb = jnp.sum(lam * (d_t * x_t)[None, :], axis=1)
            acc = acc + lam * prev_t * dec * d_t[None, :]
            return (dec * lam, acc), (gx, gdelta, gb)

        (_, grad_a), (gx_g, gdelta_g, gb_rows) = lax.scan(
            backward, (zero_state, zero_state), (d_g, x_g, b_rows, c_rows, dy_g, previous), reverse=True)
        return y_g, gx_g, gdelta_g, grad_a, gb_rows.T, grad_c_part

    outs = lax.map(group, jnp.arange(N_CHAN, dtype=jnp.int32))
    y_all, gx_all, gdelta_all, grad_a_all, gb_all, gc_all = outs

    def join(stack):
        return jnp.transpose(stack, (1, 0, 2)).reshape(stack.shape[1], EI)

    y = join(y_all)
    grad_input = join(gx_all).astype(jnp.bfloat16)
    grad_delta = join(gdelta_all)
    grad_a = jnp.transpose(grad_a_all, (1, 0, 2)).reshape(DS, EI)
    grad_rates = grad_a * a_neg
    grad_write = jnp.sum(gb_all, axis=0)
    grad_read = jnp.sum(gc_all, axis=0)
    grad_skip = jnp.sum(dy * xf, axis=0)
    gated = (y * gate_silu).astype(jnp.bfloat16)
    grad_weight = jnp.dot(gated.T, out_cotangent, preferred_element_type=jnp.float32)
    grad_gate = (dg * y * gate_sig * (1.0 + zf * (1.0 - gate_sig))).astype(jnp.bfloat16)
    grad_step = (grad_delta * jax.nn.sigmoid(step_raw.astype(jnp.float32))).astype(jnp.bfloat16)
    return (grad_input, grad_gate, grad_step, grad_rates, grad_skip, grad_write, grad_read, grad_weight)
```

```python
import functools

import jax
import jax.numpy as jnp
from jax import lax
from jax.experimental import pallas as pl
from jax.experimental.pallas import tpu as pltpu
from jax.sharding import PartitionSpec as P

CHUNK = 16
LANES = 128
LOG2E = 1.4426950408889634


def lane_groups(width):
    return [(lo, min(lo + LANES, width)) for lo in range(0, width, LANES)]


def softplus(raw):
    return jnp.maximum(raw, 0.0) + jnp.log1p(jnp.exp(-jnp.abs(raw)))


def sigmoid(value):
    return 1.0 / (1.0 + jnp.exp(-value))


def chunk_mask(rows, cols, states):
    row = lax.broadcasted_iota(jnp.int32, (rows, cols), 0)
    col = lax.broadcasted_iota(jnp.int32, (rows, cols), 1)
    return row == col // states


def wide(row, states):
    return jnp.broadcast_to(row, (states, row.shape[1]))


def end_kernel(raw_ref, x_ref, a2_ref, b_ref, out_ref, delta_s, dx_s, h_s, sum_s):
    states, width = h_s.shape
    block = raw_ref.shape[0]

    @pl.when(pl.program_id(0) == 0)
    def _():
        h_s[...] = jnp.zeros_like(h_s)
        sum_s[...] = jnp.zeros_like(sum_s)

    def chunk(c, _):
        base = pl.multiple_of(c * CHUNK, CHUNK)
        tok = pl.ds(base, CHUNK)
        delta = softplus(raw_ref[tok, :].astype(jnp.float32))
        delta_s[...] = delta
        dx_s[...] = delta * x_ref[tok, :].astype(jnp.float32)
        sum_s[...] += jnp.broadcast_to(jnp.sum(delta, axis=0, keepdims=True), sum_s.shape)
        for lo, hi in lane_groups(width):
            h = h_s[:, lo:hi]
            a2 = a2_ref[:, lo:hi]
            for k in range(CHUNK):
                d = wide(delta_s[k : k + 1, lo:hi], states)
                dx = wide(dx_s[k : k + 1, lo:hi], states)
                b = b_ref[pl.ds(pl.multiple_of((base + k) * states, states), states), : hi - lo]
                h = jnp.exp2(d * a2) * h + b * dx
            h_s[:, lo:hi] = h
        return 0

    lax.fori_loop(0, block // CHUNK, chunk, 0)

    @pl.when(pl.program_id(0) == pl.num_programs(0) - 1)
    def _():
        out_ref[:states] = h_s[...]
        out_ref[states:] = sum_s[...]


def forward_kernel(
    raw_ref, x_ref, gate_ref, dg_ref, a2_ref, b_ref, c_ref, cm_ref, skip_ref, hin_ref,
    gated_ref, ggate_ref, hprev_ref, read_ref, first_ref, gskip_ref,
    delta_s, dx_s, dy_s, hs_s, h_s, p_s, acc_s,
):
    states, width = h_s.shape
    block = raw_ref.shape[0]

    @pl.when(pl.program_id(0) == 0)
    def _():
        h_s[...] = hin_ref[...]
        p_s[...] = jnp.ones_like(p_s)
        acc_s[...] = jnp.zeros_like(acc_s)
        gskip_ref[...] = jnp.zeros_like(gskip_ref)

    mask = chunk_mask(CHUNK, CHUNK * states, states)

    def chunk(c, _):
        base = pl.multiple_of(c * CHUNK, CHUNK)
        tok = pl.ds(base, CHUNK)
        delta = softplus(raw_ref[tok, :].astype(jnp.float32))
        xf = x_ref[tok, :].astype(jnp.float32)
        delta_s[...] = delta
        dx_s[...] = delta * xf
        z = gate_ref[tok, :].astype(jnp.float32)
        s = sigmoid(z)
        dy = dg_ref[tok, :] * (z * s)
        dy_s[...] = dy
        gskip_ref[...] += jnp.sum(dy * xf, axis=0, keepdims=True)
        for lo, hi in lane_groups(width):
            h = h_s[:, lo:hi]
            p = p_s[:, lo:hi]
            acc = acc_s[:, lo:hi]
            a2 = a2_ref[:, lo:hi]
            hb = h.astype(jnp.bfloat16)
            for k in range(CHUNK):
                rows = pl.ds(pl.multiple_of((base + k) * states, states), states)
                d = wide(delta_s[k : k + 1, lo:hi], states)
                dx = wide(dx_s[k : k + 1, lo:hi], states)
                dyr = wide(dy_s[k : k + 1, lo:hi], states)
                hprev_ref[rows, lo:hi] = hb
                decay = jnp.exp2(d * a2)
                h = decay * h + b_ref[rows, : hi - lo] * dx
                hb = h.astype(jnp.bfloat16)
                hs_s[k * states : (k + 1) * states, lo:hi] = hb
                p = p * decay
                acc = acc + p * (c_ref[rows, : hi - lo] * dyr)
            h_s[:, lo:hi] = h
            p_s[:, lo:hi] = p
            acc_s[:, lo:hi] = acc
        hs = hs_s[...]
        y = jnp.dot(cm_ref[tok, :], hs, preferred_element_type=jnp.float32)
        y = y + skip_ref[...] * x_ref[tok, :].astype(jnp.float32)
        read = lax.dot_general(
            dy_s[...].astype(jnp.bfloat16), hs, (((1,), (1,)), ((), ())),
            preferred_element_type=jnp.float32,
        )
        read_ref[c] = jnp.sum(jnp.where(mask, read, 0.0), axis=0, keepdims=True)
        z = gate_ref[tok, :].astype(jnp.float32)
        s = sigmoid(z)
        gated_ref[tok, :] = (y * (z * s)).astype(jnp.bfloat16)
        ggate_ref[tok, :] = (dg_ref[tok, :] * y * s * (1.0 + z * (1.0 - s))).astype(jnp.bfloat16)
        return 0

    lax.fori_loop(0, block // CHUNK, chunk, 0)

    @pl.when(pl.program_id(0) == pl.num_programs(0) - 1)
    def _():
        first_ref[...] = acc_s[...]


def back_kernel(
    raw_ref, x_ref, gate_ref, dg_ref, a2_ref, a_ref, c_ref, bm_ref, skip_ref, hprev_ref, om_ref,
    gx_ref, gstep_ref, write_ref, rates_ref,
    delta_s, dx_s, dy_s, lam_s, wa_s, om_s, acc_s,
):
    states, width = om_s.shape
    block = raw_ref.shape[0]

    @pl.when(pl.program_id(0) == 0)
    def _():
        om_s[...] = om_ref[...]
        acc_s[...] = jnp.zeros_like(acc_s)

    mask = chunk_mask(CHUNK, CHUNK * states, states)
    ones = mask.astype(jnp.float32).astype(jnp.bfloat16)
    nchunks = block // CHUNK

    def chunk(i, _):
        c = nchunks - 1 - i
        base = pl.multiple_of(c * CHUNK, CHUNK)
        tok = pl.ds(base, CHUNK)
        delta = softplus(raw_ref[tok, :].astype(jnp.float32))
        delta_s[...] = delta
        dx_s[...] = delta * x_ref[tok, :].astype(jnp.float32)
        z = gate_ref[tok, :].astype(jnp.float32)
        dy_s[...] = dg_ref[tok, :] * (z * sigmoid(z))
        for lo, hi in lane_groups(width):
            om = om_s[:, lo:hi]
            acc = acc_s[:, lo:hi]
            a2 = a2_ref[:, lo:hi]
            a = a_ref[:, lo:hi]
            for k in reversed(range(CHUNK)):
                rows = pl.ds(pl.multiple_of((base + k) * states, states), states)
                d = wide(delta_s[k : k + 1, lo:hi], states)
                dyr = wide(dy_s[k : k + 1, lo:hi], states)
                lam = c_ref[rows, : hi - lo] * dyr + om
                lam_s[k * states : (k + 1) * states, lo:hi] = lam.astype(jnp.bfloat16)
                om = jnp.exp2(d * a2) * lam
                w = om * hprev_ref[rows, lo:hi].astype(jnp.float32)
                wa_s[k * states : (k + 1) * states, lo:hi] = (w * a).astype(jnp.bfloat16)
                acc = acc + w * d
            om_s[:, lo:hi] = om
            acc_s[:, lo:hi] = acc
        lam_all = lam_s[...]
        lam_b = jnp.dot(bm_ref[tok, :], lam_all, preferred_element_type=jnp.float32)
        rate = jnp.dot(ones, wa_s[...], preferred_element_type=jnp.float32)
        write = lax.dot_general(
            dx_s[...].astype(jnp.bfloat16), lam_all, (((1,), (1,)), ((), ())),
            preferred_element_type=jnp.float32,
        )
        write_ref[c] = jnp.sum(jnp.where(mask, write, 0.0), axis=0, keepdims=True)
        gdelta = x_ref[tok, :].astype(jnp.float32) * lam_b + rate
        gstep_ref[tok, :] = (gdelta * sigmoid(raw_ref[tok, :].astype(jnp.float32))).astype(jnp.bfloat16)
        gx_ref[tok, :] = (delta_s[...] * lam_b + dy_s[...] * skip_ref[...]).astype(jnp.bfloat16)
        return 0

    lax.fori_loop(0, nchunks, chunk, 0)

    @pl.when(pl.program_id(0) == pl.num_programs(0) - 1)
    def _():
        rates_ref[...] = acc_s[...] * a_ref[...]


def on_device(
    scan_input, gate_input, step_raw, log_rates, skip_gain,
    state_write, state_read, out_weight, out_cotangent,
):
    tokens, width = scan_input.shape
    states = log_rates.shape[0]
    block = min(64, tokens)
    nblocks = tokens // block
    f32, bf16 = jnp.float32, jnp.bfloat16
    seq_devices = lax.axis_size("seq")
    me = lax.axis_index("seq")

    a_neg = -jnp.exp(log_rates)
    a2 = a_neg * LOG2E
    skip_row = skip_gain[None, :]
    b_rows, c_rows = state_write.T, state_read.T

    def lanes(rows):
        return jnp.broadcast_to(rows[:, :, None], (tokens, states, LANES)).reshape(tokens * states, LANES)

    def diagonal(rows):
        spread = jnp.tile(rows.astype(bf16), (1, CHUNK))
        place = (jnp.arange(CHUNK * states) // states)[None, :]
        return jnp.where(place == (jnp.arange(tokens) % CHUNK)[:, None], spread, jnp.zeros((), bf16))

    b_wide, c_wide = lanes(b_rows), lanes(c_rows)
    bm, cm = diagonal(b_rows), diagonal(c_rows)

    def specs(order):
        by_token = pl.BlockSpec((block, width), lambda i: (order(i), 0))
        by_state = pl.BlockSpec((block * states, LANES), lambda i: (order(i), 0))
        history = pl.BlockSpec((block * states, width), lambda i: (order(i), 0))
        diag = pl.BlockSpec((block, CHUNK * states), lambda i: (order(i), 0))
        sums = pl.BlockSpec((block // CHUNK, 1, CHUNK * states), lambda i: (order(i), 0, 0))
        return by_token, by_state, history, diag, sums

    state_spec = pl.BlockSpec((states, width), lambda i: (0, 0))
    row_spec = pl.BlockSpec((1, width), lambda i: (0, 0))
    params = pltpu.CompilerParams(dimension_semantics=("arbitrary",))
    token_scratch = pltpu.VMEM((CHUNK, width), f32)
    state_scratch = pltpu.VMEM((states, width), f32)
    chunk_scratch = pltpu.VMEM((CHUNK * states, width), bf16)
    volume = tokens * states * width

    def cost(scale):
        return pl.CostEstimate(flops=scale * volume, bytes_accessed=4 * volume, transcendentals=volume)

    by_token, by_state, history, diag, sums = specs(lambda i: i)
    pad = 8
    ending = pl.pallas_call(
        end_kernel,
        grid=(nblocks,),
        in_specs=[by_token, by_token, state_spec, by_state],
        out_specs=pl.BlockSpec((states + pad, width), lambda i: (0, 0)),
        out_shape=jax.ShapeDtypeStruct((states + pad, width), f32),
        scratch_shapes=[token_scratch, token_scratch, state_scratch, pltpu.VMEM((pad, width), f32)],
        compiler_params=params,
        cost_estimate=cost(5),
        name="ending",
    )(step_raw, scan_input, a2, b_wide)

    dout_full = lax.all_gather(out_cotangent, "chan", axis=1, tiled=True)
    endings = lax.all_gather(ending, "seq", axis=0)
    decays = jnp.exp2(endings[:, states : states + 1] * a2[None])
    h_in = jnp.zeros((states, width), f32)
    for j in range(seq_devices - 1):
        h_in = jnp.where(j < me, decays[j] * h_in + endings[j, :states], h_in)

    dg = lax.dot_general(dout_full, out_weight, (((1,), (1,)), ((), ())), preferred_element_type=f32)

    gated, grad_gate, hprev, read, first, skip_part = pl.pallas_call(
        forward_kernel,
        grid=(nblocks,),
        in_specs=[by_token] * 4 + [state_spec, by_state, by_state, diag, row_spec, state_spec],
        out_specs=[by_token, by_token, history, sums, state_spec, row_spec],
        out_shape=[
            jax.ShapeDtypeStruct((tokens, width), bf16),
            jax.ShapeDtypeStruct((tokens, width), bf16),
            jax.ShapeDtypeStruct((tokens * states, width), bf16),
            jax.ShapeDtypeStruct((tokens // CHUNK, 1, CHUNK * states), f32),
            jax.ShapeDtypeStruct((states, width), f32),
            jax.ShapeDtypeStruct((1, width), f32),
        ],
        scratch_shapes=[token_scratch] * 3 + [chunk_scratch] + [state_scratch] * 3,
        compiler_params=params,
        cost_estimate=cost(12),
        name="forward",
    )(step_raw, scan_input, gate_input, dg, a2, b_wide, c_wide, cm, skip_row, h_in)

    firsts = lax.all_gather(first, "seq", axis=0)
    gated_all = lax.all_gather(gated, "seq", axis=0, tiled=True)
    columns = lax.all_to_all(dout_full, "seq", split_axis=1, concat_axis=0, tiled=True)
    omega = jnp.zeros((states, width), f32)
    for j in reversed(range(1, seq_devices)):
        omega = jnp.where(j > me, decays[j] * omega + firsts[j], omega)

    by_token, by_state, history, diag, sums = specs(lambda i: nblocks - 1 - i)
    grad_input, grad_step, write, rates = pl.pallas_call(
        back_kernel,
        grid=(nblocks,),
        in_specs=[by_token] * 4
        + [state_spec, state_spec, by_state, diag, row_spec, history, state_spec],
        out_specs=[by_token, by_token, sums, state_spec],
        out_shape=[
            jax.ShapeDtypeStruct((tokens, width), bf16),
            jax.ShapeDtypeStruct((tokens, width), bf16),
            jax.ShapeDtypeStruct((tokens // CHUNK, 1, CHUNK * states), f32),
            jax.ShapeDtypeStruct((states, width), f32),
        ],
        scratch_shapes=[token_scratch] * 3 + [chunk_scratch] * 2 + [state_scratch] * 2,
        compiler_params=params,
        cost_estimate=cost(14),
        name="backward",
    )(step_raw, scan_input, gate_input, dg, a2, a_neg, c_wide, bm, skip_row, hprev, omega)

    both = jnp.concatenate([write.reshape(tokens, states).T, read.reshape(tokens, states).T], axis=0)
    both = lax.psum_scatter(both, "chan", scatter_dimension=1, tiled=True)
    grad_write, grad_read = both[:states], both[states:]
    sums_seq = lax.psum(jnp.concatenate([rates, skip_part], axis=0), "seq")
    grad_rates, grad_skip = sums_seq[:states], sums_seq[states]
    grad_weight = lax.dot_general(
        gated_all, columns, (((0,), (0,)), ((), ())), preferred_element_type=f32
    )
    return (
        grad_input, grad_gate, grad_step, grad_rates, grad_skip, grad_write, grad_read, grad_weight,
    )


def solution(mesh):
    return jax.shard_map(
        on_device,
        mesh=mesh,
        in_specs=(
            P("seq", "chan"),
            P("seq", "chan"),
            P("seq", "chan"),
            P(None, "chan"),
            P("chan"),
            P(None, "seq"),
            P(None, "seq"),
            P("chan", None),
            P("seq", "chan"),
        ),
        out_specs=(
            P("seq", "chan"),
            P("seq", "chan"),
            P("seq", "chan"),
            P(None, "chan"),
            P("chan"),
            P(None, ("seq", "chan")),
            P(None, ("seq", "chan")),
            P("chan", "seq"),
        ),
        check_vma=False,
    )
```

```python
import functools

import jax
import jax.numpy as jnp
from jax import lax
from jax.experimental import pallas as pl
from jax.experimental.pallas import tpu as pltpu
from jax.sharding import PartitionSpec as P

CHUNK = 16
LANES = 128
LOG2E = 1.4426950408889634


def lane_groups(width):
    return [(lo, min(lo + LANES, width)) for lo in range(0, width, LANES)]


def softplus(raw):
    return jnp.maximum(raw, 0.0) + jnp.log1p(jnp.exp(-jnp.abs(raw)))


def sigmoid(value):
    return 1.0 / (1.0 + jnp.exp(-value))


def from_all(array, axis):
    copies = jnp.broadcast_to(array[None], (lax.axis_size(axis),) + array.shape)
    return lax.all_to_all(copies, axis, split_axis=0, concat_axis=0, tiled=True)


def chunk_mask(rows, cols, states):
    row = lax.broadcasted_iota(jnp.int32, (rows, cols), 0)
    col = lax.broadcasted_iota(jnp.int32, (rows, cols), 1)
    return row == col // states


def wide(row, states):
    return jnp.broadcast_to(row, (states, row.shape[1]))


def end_kernel(raw_ref, x_ref, a2_ref, b_ref, out_ref, delta_s, dx_s, h_s, sum_s):
    states, width = h_s.shape
    block = raw_ref.shape[0]

    @pl.when(pl.program_id(0) == 0)
    def _():
        h_s[...] = jnp.zeros_like(h_s)
        sum_s[...] = jnp.zeros_like(sum_s)

    def chunk(c, _):
        base = pl.multiple_of(c * CHUNK, CHUNK)
        tok = pl.ds(base, CHUNK)
        delta = softplus(raw_ref[tok, :].astype(jnp.float32))
        delta_s[...] = delta
        dx_s[...] = delta * x_ref[tok, :].astype(jnp.float32)
        sum_s[...] += jnp.broadcast_to(jnp.sum(delta, axis=0, keepdims=True), sum_s.shape)
        for lo, hi in lane_groups(width):
            h = h_s[:, lo:hi]
            a2 = a2_ref[:, lo:hi]
            for k in range(CHUNK):
                d = wide(delta_s[k : k + 1, lo:hi], states)
                dx = wide(dx_s[k : k + 1, lo:hi], states)
                b = b_ref[pl.ds(pl.multiple_of((base + k) * states, states), states), : hi - lo]
                h = jnp.exp2(d * a2) * h + b * dx
            h_s[:, lo:hi] = h
        return 0

    lax.fori_loop(0, block // CHUNK, chunk, 0)

    @pl.when(pl.program_id(0) == pl.num_programs(0) - 1)
    def _():
        out_ref[:states] = h_s[...]
        out_ref[states:] = sum_s[...]


def forward_kernel(
    raw_ref, x_ref, gate_ref, dg_ref, a2_ref, b_ref, c_ref, cm_ref, skip_ref, hin_ref,
    gated_ref, ggate_ref, hprev_ref, read_ref, first_ref, gskip_ref,
    delta_s, dx_s, dy_s, hs_s, h_s, p_s, acc_s,
):
    states, width = h_s.shape
    block = raw_ref.shape[0]

    @pl.when(pl.program_id(0) == 0)
    def _():
        h_s[...] = hin_ref[...]
        p_s[...] = jnp.ones_like(p_s)
        acc_s[...] = jnp.zeros_like(acc_s)
        gskip_ref[...] = jnp.zeros_like(gskip_ref)

    mask = chunk_mask(CHUNK, CHUNK * states, states)

    def chunk(c, _):
        base = pl.multiple_of(c * CHUNK, CHUNK)
        tok = pl.ds(base, CHUNK)
        delta = softplus(raw_ref[tok, :].astype(jnp.float32))
        xf = x_ref[tok, :].astype(jnp.float32)
        delta_s[...] = delta
        dx_s[...] = delta * xf
        z = gate_ref[tok, :].astype(jnp.float32)
        s = sigmoid(z)
        dy = dg_ref[tok, :] * (z * s)
        dy_s[...] = dy
        gskip_ref[...] += jnp.sum(dy * xf, axis=0, keepdims=True)
        for lo, hi in lane_groups(width):
            h = h_s[:, lo:hi]
            p = p_s[:, lo:hi]
            acc = acc_s[:, lo:hi]
            a2 = a2_ref[:, lo:hi]
            hb = h.astype(jnp.bfloat16)
            for k in range(CHUNK):
                rows = pl.ds(pl.multiple_of((base + k) * states, states), states)
                d = wide(delta_s[k : k + 1, lo:hi], states)
                dx = wide(dx_s[k : k + 1, lo:hi], states)
                dyr = wide(dy_s[k : k + 1, lo:hi], states)
                hprev_ref[rows, lo:hi] = hb
                decay = jnp.exp2(d * a2)
                h = decay * h + b_ref[rows, : hi - lo] * dx
                hb = h.astype(jnp.bfloat16)
                hs_s[k * states : (k + 1) * states, lo:hi] = hb
                p = p * decay
                acc = acc + p * (c_ref[rows, : hi - lo] * dyr)
            h_s[:, lo:hi] = h
            p_s[:, lo:hi] = p
            acc_s[:, lo:hi] = acc
        hs = hs_s[...]
        y = jnp.dot(cm_ref[tok, :], hs, preferred_element_type=jnp.float32)
        y = y + skip_ref[...] * x_ref[tok, :].astype(jnp.float32)
        read = lax.dot_general(
            dy_s[...].astype(jnp.bfloat16), hs, (((1,), (1,)), ((), ())),
            preferred_element_type=jnp.float32,
        )
        read_ref[c] = jnp.sum(jnp.where(mask, read, 0.0), axis=0, keepdims=True)
        z = gate_ref[tok, :].astype(jnp.float32)
        s = sigmoid(z)
        gated_ref[tok, :] = (y * (z * s)).astype(jnp.bfloat16)
        ggate_ref[tok, :] = (dg_ref[tok, :] * y * s * (1.0 + z * (1.0 - s))).astype(jnp.bfloat16)
        return 0

    lax.fori_loop(0, block // CHUNK, chunk, 0)

    @pl.when(pl.program_id(0) == pl.num_programs(0) - 1)
    def _():
        first_ref[...] = acc_s[...]


def back_kernel(
    raw_ref, x_ref, gate_ref, dg_ref, a2_ref, a_ref, c_ref, bm_ref, skip_ref, hprev_ref, om_ref,
    gx_ref, gstep_ref, write_ref, rates_ref,
    delta_s, dx_s, dy_s, lam_s, wa_s, om_s, acc_s,
):
    states, width = om_s.shape
    block = raw_ref.shape[0]

    @pl.when(pl.program_id(0) == 0)
    def _():
        om_s[...] = om_ref[...]
        acc_s[...] = jnp.zeros_like(acc_s)

    mask = chunk_mask(CHUNK, CHUNK * states, states)
    ones = mask.astype(jnp.float32).astype(jnp.bfloat16)
    nchunks = block // CHUNK

    def chunk(i, _):
        c = nchunks - 1 - i
        base = pl.multiple_of(c * CHUNK, CHUNK)
        tok = pl.ds(base, CHUNK)
        delta = softplus(raw_ref[tok, :].astype(jnp.float32))
        delta_s[...] = delta
        dx_s[...] = delta * x_ref[tok, :].astype(jnp.float32)
        z = gate_ref[tok, :].astype(jnp.float32)
        dy_s[...] = dg_ref[tok, :] * (z * sigmoid(z))
        for lo, hi in lane_groups(width):
            om = om_s[:, lo:hi]
            acc = acc_s[:, lo:hi]
            a2 = a2_ref[:, lo:hi]
            a = a_ref[:, lo:hi]
            for k in reversed(range(CHUNK)):
                rows = pl.ds(pl.multiple_of((base + k) * states, states), states)
                d = wide(delta_s[k : k + 1, lo:hi], states)
                dyr = wide(dy_s[k : k + 1, lo:hi], states)
                lam = c_ref[rows, : hi - lo] * dyr + om
                lam_s[k * states : (k + 1) * states, lo:hi] = lam.astype(jnp.bfloat16)
                om = jnp.exp2(d * a2) * lam
                w = om * hprev_ref[rows, lo:hi].astype(jnp.float32)
                wa_s[k * states : (k + 1) * states, lo:hi] = (w * a).astype(jnp.bfloat16)
                acc = acc + w * d
            om_s[:, lo:hi] = om
            acc_s[:, lo:hi] = acc
        lam_all = lam_s[...]
        lam_b = jnp.dot(bm_ref[tok, :], lam_all, preferred_element_type=jnp.float32)
        rate = jnp.dot(ones, wa_s[...], preferred_element_type=jnp.float32)
        write = lax.dot_general(
            dx_s[...].astype(jnp.bfloat16), lam_all, (((1,), (1,)), ((), ())),
            preferred_element_type=jnp.float32,
        )
        write_ref[c] = jnp.sum(jnp.where(mask, write, 0.0), axis=0, keepdims=True)
        gdelta = x_ref[tok, :].astype(jnp.float32) * lam_b + rate
        gstep_ref[tok, :] = (gdelta * sigmoid(raw_ref[tok, :].astype(jnp.float32))).astype(jnp.bfloat16)
        gx_ref[tok, :] = (delta_s[...] * lam_b + dy_s[...] * skip_ref[...]).astype(jnp.bfloat16)
        return 0

    lax.fori_loop(0, nchunks, chunk, 0)

    @pl.when(pl.program_id(0) == pl.num_programs(0) - 1)
    def _():
        rates_ref[...] = acc_s[...] * a_ref[...]


def on_device(
    scan_input, gate_input, step_raw, log_rates, skip_gain,
    state_write, state_read, out_weight, out_cotangent,
):
    tokens, width = scan_input.shape
    states = log_rates.shape[0]
    block = min(64, tokens)
    nblocks = tokens // block
    f32, bf16 = jnp.float32, jnp.bfloat16
    seq_devices = lax.axis_size("seq")
    me = lax.axis_index("seq")

    a_neg = -jnp.exp(log_rates)
    a2 = a_neg * LOG2E
    skip_row = skip_gain[None, :]
    b_rows, c_rows = state_write.T, state_read.T

    def lanes(rows):
        return jnp.broadcast_to(rows[:, :, None], (tokens, states, LANES)).reshape(tokens * states, LANES)

    def diagonal(rows):
        spread = jnp.tile(rows.astype(bf16), (1, CHUNK))
        place = (jnp.arange(CHUNK * states) // states)[None, :]
        return jnp.where(place == (jnp.arange(tokens) % CHUNK)[:, None], spread, jnp.zeros((), bf16))

    b_wide, c_wide = lanes(b_rows), lanes(c_rows)
    bm, cm = diagonal(b_rows), diagonal(c_rows)

    def specs(order):
        by_token = pl.BlockSpec((block, width), lambda i: (order(i), 0))
        by_state = pl.BlockSpec((block * states, LANES), lambda i: (order(i), 0))
        history = pl.BlockSpec((block * states, width), lambda i: (order(i), 0))
        diag = pl.BlockSpec((block, CHUNK * states), lambda i: (order(i), 0))
        sums = pl.BlockSpec((block // CHUNK, 1, CHUNK * states), lambda i: (order(i), 0, 0))
        return by_token, by_state, history, diag, sums

    state_spec = pl.BlockSpec((states, width), lambda i: (0, 0))
    row_spec = pl.BlockSpec((1, width), lambda i: (0, 0))
    params = pltpu.CompilerParams(dimension_semantics=("arbitrary",))
    token_scratch = pltpu.VMEM((CHUNK, width), f32)
    state_scratch = pltpu.VMEM((states, width), f32)
    chunk_scratch = pltpu.VMEM((CHUNK * states, width), bf16)
    volume = tokens * states * width

    def cost(scale):
        return pl.CostEstimate(flops=scale * volume, bytes_accessed=4 * volume, transcendentals=volume)

    by_token, by_state, history, diag, sums = specs(lambda i: i)
    pad = 8
    ending = pl.pallas_call(
        end_kernel,
        grid=(nblocks,),
        in_specs=[by_token, by_token, state_spec, by_state],
        out_specs=pl.BlockSpec((states + pad, width), lambda i: (0, 0)),
        out_shape=jax.ShapeDtypeStruct((states + pad, width), f32),
        scratch_shapes=[token_scratch, token_scratch, state_scratch, pltpu.VMEM((pad, width), f32)],
        compiler_params=params,
        cost_estimate=cost(5),
        name="ending",
    )(step_raw, scan_input, a2, b_wide)

    dout_full = jnp.swapaxes(from_all(out_cotangent, "chan"), 0, 1).reshape(tokens, -1)
    endings = from_all(ending, "seq")
    decays = jnp.exp2(endings[:, states : states + 1] * a2[None])
    h_in = jnp.zeros((states, width), f32)
    for j in range(seq_devices - 1):
        h_in = jnp.where(j < me, decays[j] * h_in + endings[j, :states], h_in)

    dg = lax.dot_general(dout_full, out_weight, (((1,), (1,)), ((), ())), preferred_element_type=f32)

    gated, grad_gate, hprev, read, first, skip_part = pl.pallas_call(
        forward_kernel,
        grid=(nblocks,),
        in_specs=[by_token] * 4 + [state_spec, by_state, by_state, diag, row_spec, state_spec],
        out_specs=[by_token, by_token, history, sums, state_spec, row_spec],
        out_shape=[
            jax.ShapeDtypeStruct((tokens, width), bf16),
            jax.ShapeDtypeStruct((tokens, width), bf16),
            jax.ShapeDtypeStruct((tokens * states, width), bf16),
            jax.ShapeDtypeStruct((tokens // CHUNK, 1, CHUNK * states), f32),
            jax.ShapeDtypeStruct((states, width), f32),
            jax.ShapeDtypeStruct((1, width), f32),
        ],
        scratch_shapes=[token_scratch] * 3 + [chunk_scratch] + [state_scratch] * 3,
        compiler_params=params,
        cost_estimate=cost(12),
        name="forward",
    )(step_raw, scan_input, gate_input, dg, a2, b_wide, c_wide, cm, skip_row, h_in)

    firsts = from_all(first, "seq")
    gated_all = from_all(gated, "seq").reshape(-1, width)
    columns = lax.all_to_all(dout_full, "seq", split_axis=1, concat_axis=0, tiled=True)
    omega = jnp.zeros((states, width), f32)
    for j in reversed(range(1, seq_devices)):
        omega = jnp.where(j > me, decays[j] * omega + firsts[j], omega)

    by_token, by_state, history, diag, sums = specs(lambda i: nblocks - 1 - i)
    grad_input, grad_step, write, rates = pl.pallas_call(
        back_kernel,
        grid=(nblocks,),
        in_specs=[by_token] * 4
        + [state_spec, state_spec, by_state, diag, row_spec, history, state_spec],
        out_specs=[by_token, by_token, sums, state_spec],
        out_shape=[
            jax.ShapeDtypeStruct((tokens, width), bf16),
            jax.ShapeDtypeStruct((tokens, width), bf16),
            jax.ShapeDtypeStruct((tokens // CHUNK, 1, CHUNK * states), f32),
            jax.ShapeDtypeStruct((states, width), f32),
        ],
        scratch_shapes=[token_scratch] * 3 + [chunk_scratch] * 2 + [state_scratch] * 2,
        compiler_params=params,
        cost_estimate=cost(14),
        name="backward",
    )(step_raw, scan_input, gate_input, dg, a2, a_neg, c_wide, bm, skip_row, hprev, omega)

    both = jnp.concatenate([write.reshape(tokens, states).T, read.reshape(tokens, states).T], axis=0)
    chan_devices = lax.axis_size("chan")
    pieces = jnp.swapaxes(both.reshape(2 * states, chan_devices, -1), 0, 1)
    both = jnp.sum(lax.all_to_all(pieces, "chan", split_axis=0, concat_axis=0, tiled=True), axis=0)
    grad_write, grad_read = both[:states], both[states:]
    sums_seq = jnp.sum(from_all(jnp.concatenate([rates, skip_part], axis=0), "seq"), axis=0)
    grad_rates, grad_skip = sums_seq[:states], sums_seq[states]
    grad_weight = lax.dot_general(
        gated_all, columns, (((0,), (0,)), ((), ())), preferred_element_type=f32
    )
    return (
        grad_input, grad_gate, grad_step, grad_rates, grad_skip, grad_write, grad_read, grad_weight,
    )


def solution(mesh):
    return jax.shard_map(
        on_device,
        mesh=mesh,
        in_specs=(
            P("seq", "chan"),
            P("seq", "chan"),
            P("seq", "chan"),
            P(None, "chan"),
            P("chan"),
            P(None, "seq"),
            P(None, "seq"),
            P("chan", None),
            P("seq", "chan"),
        ),
        out_specs=(
            P("seq", "chan"),
            P("seq", "chan"),
            P("seq", "chan"),
            P(None, "chan"),
            P("chan"),
            P(None, ("seq", "chan")),
            P(None, ("seq", "chan")),
            P("chan", "seq"),
        ),
        check_vma=False,
    )
```
